32 devices in a mesh: rows: 8 (over z, core), tiles: 4 (over y, x).
Axes of the slice: x: 2, y: 2, z: 4, core: 2. Of those that a mesh axis runs over, the one named last changes fastest.
Arguments:
- features: bfloat16 [4096, 16384], P(('rows', 'tiles')), as said below
- row_salt: int32 [4096], P(('rows', 'tiles')), may hold values from 0 to 32767
- column_multiplier: int32 [16384], replicated, may hold values from 1 to 32767
- column_offset: int32 [16384], replicated, may hold values from 0 to 65520
- thresholds: int32 [16384], replicated, may hold values from 16000 to 65520
Outputs:
- similarity: float32 [256, 16384], P('rows', 'tiles')
The draws below stay inside these ranges and needn't reach their ends.
Inputs may be any that keep to these rules, and one draw needn't show every extreme that they name: `features`: Real-valued entries of order one.
All inputs are finite; a program needn't handle non-finite values.
Results may differ from the reference program's by a relative error of at most 0.0028.
Values sent between devices are 32-bit elements; how exact they have to be, the bound alone decides.
A program may use at most 64 MiB of HBM per device.

```python
import jax
import jax.numpy as jnp
from jax import lax

N = 16384
WIN = 256
ROWS_DEV = 128
ROWS = 4096


def draw_features(key, part):
    keys = jax.random.split(jax.random.fold_in(key, 11), 5)
    position = jnp.arange(ROWS, dtype=jnp.float32) / ROWS
    rough = jnp.exp(jax.random.uniform(keys[0], (ROWS,), jnp.float32, 0.0, 2.3))
    row_scale = (1.0 + 2.0 * position) * rough / 3.0
    col_scale = jnp.exp(jax.random.uniform(keys[1], (N,), jnp.float32, 0.0, 2.3)) / 3.0
    factors = jax.random.normal(keys[2], (ROWS, 8), jnp.float32)
    loads = 0.35 * jax.random.normal(keys[3], (8, N), jnp.float32)
    noise = jax.random.normal(keys[4], (ROWS, N), jnp.float32)
    values = (noise + jnp.dot(factors, loads)) * row_scale[:, None] * col_scale[None, :]
    return jnp.clip(values, -8.0, 8.0).astype(jnp.bfloat16)


def place_ends(result, own_key, low, largest):
    longest = result.shape.index(max(result.shape))
    spots = []
    for shift in (0, 1):
        where = [jax.random.randint(jax.random.fold_in(own_key, axis), (), 0, length) for axis, length in enumerate(result.shape)]
        where[longest] = (where[longest] + shift) % result.shape[longest]
        spots.append(tuple(where))
    return result.at[spots[0]].set(low).at[spots[1]].set(largest)


def setup_inputs(seed: int = 0) -> dict:
    splits = jax.random.split(jax.random.key(seed), 6)
    features = draw_features(jax.random.fold_in(splits[5], 71), 0)
    row_salt = place_ends(jax.random.randint(splits[1], (ROWS,), 0, 32768), jax.random.fold_in(splits[1], 1), 0, 32767).astype(jnp.int32)
    column_multiplier = place_ends(jax.random.randint(splits[2], (N,), 1, 32768), jax.random.fold_in(splits[2], 1), 1, 32767).astype(jnp.int32)
    column_offset = place_ends(jax.random.randint(splits[3], (N,), 0, 65521), jax.random.fold_in(splits[3], 1), 0, 65520).astype(jnp.int32)
    thresholds = place_ends(jax.random.randint(splits[4], (N,), 16000, 65521), jax.random.fold_in(splits[4], 1), 16000, 65520).astype(jnp.int32)
    return {"features": features, "row_salt": row_salt, "column_multiplier": column_multiplier, "column_offset": column_offset, "thresholds": thresholds}


def sample_block(block, salts, column_multiplier, column_offset, thresholds):
    hashed = (salts[:, None] * column_multiplier[None, :] + column_offset[None, :]) % 65521
    weight = lax.rsqrt(thresholds.astype(jnp.float32) / 65521.0)
    values = block.astype(jnp.float32) * weight[None, :]
    return jnp.where(hashed < thresholds[None, :], values, jnp.zeros_like(values)).astype(jnp.bfloat16)

def reference(features, row_salt, column_multiplier, column_offset, thresholds):
    blocks = features.reshape(ROWS // ROWS_DEV, ROWS_DEV, N)
    salts = row_salt.reshape(ROWS // ROWS_DEV, ROWS_DEV)

    def step(carry, items):
        gram, squares = carry
        block, salt = items
        wide = block.astype(jnp.float32)
        squares = squares + lax.optimization_barrier(jnp.sum(wide * wide, axis=0))
        sampled = sample_block(block, salt, column_multiplier, column_offset, thresholds)
        gram = gram + jnp.dot(sampled[:, :WIN].T, sampled, preferred_element_type=jnp.float32)
        return ((gram, squares), None)
    start = (jnp.zeros((WIN, N), jnp.float32), jnp.zeros((N,), jnp.float32))
    (gram, squares), unused = lax.scan(step, start, (blocks, salts))
    norms = jnp.sqrt(squares + 1e-06)
    return gram / (norms[:WIN, None] * norms[None, :])
```

```python
import functools

import jax
import jax.numpy as jnp
from jax import lax
from jax.experimental import pallas as pl
from jax.experimental.pallas import tpu as pltpu
from jax.sharding import PartitionSpec as P

WIN = 256
PRIME = 65521
AHEAD = 2
MESH = pl.DeviceIdType.MESH


class Plan:
    def __init__(self, rows, tiles, users, columns):
        self.rows, self.tiles, self.users, self.columns = rows, tiles, users, columns
        self.outer, self.inner = 2, tiles // 2
        self.tile_cols = columns // tiles
        self.tile_rows = WIN // rows
        self.sub = self.tile_cols // 4
        self.width = min(self.sub, 256)
        self.pieces = self.sub // self.width
        self.group = (2 * self.inner, 2 * self.outer)
        self.adds = (self.outer, self.inner)


def fold(h):
    return (h >> 16) * 15 + (h & 65535)


def kernel(
    plan, feat, salt, mult, offset, thr, out, qn, cn,
    saltc, q_own, q0, q1, qt0, qt1, s0, s1, r0, r1, p0, p1, g0, g1, acc, fin, sq, sqr, sqa, sqf,
    q_send, q_recv, a_send0, a_recv0, a_send1, a_recv1, b_send0, b_recv0, b_send1, b_recv1,
    c_send, c_recv, d_send, d_recv, e_send, e_recv,
):
    R, T, users, width, K = plan.rows, plan.tiles, plan.users, plan.width, plan.pieces
    A, B, CT, sub, RB = plan.outer, plan.inner, plan.tile_cols, plan.sub, plan.tile_rows
    r, t = lax.axis_index("rows"), lax.axis_index("tiles")
    c = lax.rem(r, 2)
    base = r - c
    a, b = t // B, lax.rem(t, B)
    q_in, qt, s, rc, part, got = (q0, q1), (qt0, qt1), (s0, s1), (r0, r1), (p0, p1), (g0, g1)
    a_sem, b_sem = ((a_send0, a_recv0), (a_send1, a_recv1)), ((b_send0, b_recv0), (b_send1, b_recv1))

    def member(p, d):
        own = (b if p == 0 else a) * 2 + c
        other = lax.rem(own + d, plan.group[p])
        return other // 2, lax.rem(other, 2)

    def device(p, d):
        along, core = member(p, d)
        return (base + core, a * B + along if p == 0 else along * B + b)

    def adder(p, e):
        if p == 0:
            return (r, lax.rem(a + e, A) * B + b)
        return (r, a * B + lax.rem(b + e, B))

    def remote(src, dst, send, recv, to):
        return pltpu.make_async_remote_copy(
            src_ref=src, dst_ref=dst, send_sem=send, recv_sem=recv, device_id=to, device_id_type=MESH
        )

    def q_copy(p, d):
        i = d - 1 if p == 0 else plan.group[0] - 1 + d - 1
        return remote(q_own, q_in[p].at[d], q_send.at[i], q_recv.at[i], device(p, d))

    def a_copy(p, k, d):
        return remote(
            s[p].at[k, d - 1], rc[p].at[k, pl.ds(d * users, users)],
            a_sem[p][0].at[k, d - 1], a_sem[p][1].at[k, d - 1], device(p, d),
        )

    def b_copy(p, k, e):
        return remote(
            part[p].at[k, e], got[p].at[k, e - 1], b_sem[p][0].at[k, e - 1], b_sem[p][1].at[k, e - 1], adder(p, e)
        )

    def c_copy(p, k, d):
        other = lax.rem(r + d, R)
        return remote(
            acc.at[p, k, pl.ds(pl.multiple_of(other * RB, RB), RB)], fin.at[p, k, d - 1],
            c_send.at[p, k, d - 1], c_recv.at[p, k, d - 1], (other, t),
        )

    def d_copy(d):
        other = lax.rem(t + d, T)
        return remote(sq.at[other], sqr.at[d - 1], d_send.at[d - 1], d_recv.at[d - 1], (r, other))

    def e_copy(d):
        return remote(sqa, sqf.at[d - 1], e_send.at[d - 1], e_recv.at[d - 1], (lax.rem(r + d, R), t))

    step = min(users, 64)

    def sample(start, size, store):
        cols = pl.ds(pl.multiple_of(start, 128), size)
        by, plus, limit = mult[:, cols], offset[:, cols], thr[:, cols]
        weight = lax.rsqrt(limit.astype(jnp.float32) / float(PRIME))

        def body(i, total):
            rows = pl.ds(pl.multiple_of(i * step, step), step)
            x = feat[rows, cols].astype(jnp.float32)
            h = fold(fold(saltc[rows, :] * by + plus))
            h = jnp.where(h >= PRIME, h - PRIME, h)
            value = x * weight
            store(pl.multiple_of(i * step, step), jnp.where(h < limit, value, jnp.zeros_like(value)))
            return total + jnp.sum((x * x).reshape(step // 8, 8, size), axis=0)

        total = lax.fori_loop(0, users // step, body, jnp.zeros((8, size), jnp.float32))
        return jnp.sum(total, axis=0, keepdims=True)

    def sample_for(p, k, d, store):
        along, core = member(p, d)
        for e in range(plan.adds[p]):
            if p == 0:
                tile = lax.rem(a + e, A) * B + along
            else:
                tile = along * B + lax.rem(b + e, B)
            inside = p * (CT // 2) + core * sub + k * width
            squares = sample(tile * CT + inside, width, functools.partial(store, e))
            sq[tile, :, pl.ds(pl.multiple_of(inside, 128), width)] = squares

    def gather_piece(k):
        for p in range(2):
            def away(d, _):
                def store(e, row, value):
                    s[p][k, d - 1, pl.ds(row, step), pl.ds(e * width, width)] = value

                sample_for(p, k, d, store)
                a_copy(p, k, d).start()
                return 0

            lax.fori_loop(1, plan.group[p], away, 0)
        for p in range(2):
            def store(e, row, value):
                rc[p][k, pl.ds(row, step), pl.ds(e * width, width)] = value

            sample_for(p, k, 0, store)

    barrier = pltpu.get_barrier_semaphore()
    for d in range(1, 2 * T):
        other = lax.rem(t * 2 + c + d, 2 * T)
        pl.semaphore_signal(
            barrier, inc=1, device_id=(base + lax.rem(other, 2), other // 2), device_id_type=MESH
        )
    for d in range(1, R):
        pl.semaphore_signal(barrier, inc=1, device_id=(lax.rem(r + d, R), t), device_id_type=MESH)

    diagonal = lax.broadcasted_iota(jnp.int32, (users, users), 0) == lax.broadcasted_iota(
        jnp.int32, (users, users), 1
    )
    spread = jnp.where(diagonal, jnp.broadcast_to(salt[...].astype(jnp.float32), (users, users)), 0.0)
    saltc[...] = jnp.sum(spread, axis=1, keepdims=True).astype(jnp.int32)

    def store_q(row, value):
        q_own[pl.ds(row, step), :] = value

    q_squares = sample(0, WIN, store_q)
    for tile in range(T):
        sq[tile, :, pl.ds(CT, WIN)] = q_squares
    pl.semaphore_wait(barrier, 2 * T - 1 + R - 1)

    for p in range(2):
        for d in range(1, plan.group[p]):
            q_copy(p, d).start()
    for k in range(min(AHEAD, K)):
        gather_piece(k)
    for p in range(2):
        qt[p][:, pl.ds(0, users)] = q_own[...].T.astype(jnp.bfloat16)
        for d in range(1, plan.group[p]):
            q_copy(p, d).wait()
            qt[p][:, pl.ds(d * users, users)] = q_in[p][d].T.astype(jnp.bfloat16)

    for k in range(K + 1):
        if k < K:
            for p in range(2):
                for d in range(1, plan.group[p]):
                    a_copy(p, k, d).wait_recv()
                for e in list(range(1, plan.adds[p])) + [0]:
                    block = rc[p][k, :, pl.ds(e * width, width)].astype(jnp.bfloat16)
                    part[p][k, e] = jnp.dot(qt[p][...], block, preferred_element_type=jnp.float32)
                    if e:
                        b_copy(p, k, e).start()
        if k + AHEAD < K:
            gather_piece(k + AHEAD)
        if k == max(0, K - 1 - AHEAD):
            for d in range(1, T):
                d_copy(d).start()
        if k >= 1:
            for p in range(2):
                total = part[p][k - 1, 0]
                for e in range(1, plan.adds[p]):
                    b_copy(p, k - 1, e).wait_recv()
                    total = total + got[p][k - 1, e - 1]
                acc[p, k - 1] = total
                for d in range(1, R):
                    c_copy(p, k - 1, d).start()
        if k == K - 1:
            total = sq[t]
            for d in range(1, T):
                d_copy(d).wait_recv()
                total = total + sqr[d - 1]
            sqa[...] = total
            for d in range(1, R):
                e_copy(d).start()

    squares = sqa[...]
    for d in range(1, R):
        e_copy(d).wait_recv()
        squares = squares + sqf[d - 1]
    norms = jnp.sqrt(squares + 1e-06)
    cn[...] = norms[:, :CT]
    mine = lax.broadcasted_iota(jnp.int32, (RB, WIN), 1) == r * RB + lax.broadcasted_iota(
        jnp.int32, (RB, WIN), 0
    )
    qn[...] = jnp.sum(
        jnp.where(mine, jnp.broadcast_to(norms[:, CT:], (RB, WIN)), 0.0), axis=1, keepdims=True
    )

    for k in range(K):
        for p in range(2):
            same = acc[p, k, pl.ds(pl.multiple_of(r * RB, RB), RB)]
            cross = None
            for d in range(1, R):
                c_copy(p, k, d).wait_recv()
                piece = fin[p, k, d - 1]
                if d % 2 == 0:
                    same = same + piece
                else:
                    cross = piece if cross is None else cross + piece
            for core, value in ((c, same), (1 - c, cross)):
                start = pl.multiple_of(p * (CT // 2) + core * sub + k * width, 128)
                out[:, pl.ds(start, width)] = value

    for k in range(K):
        for p in range(2):
            for d in range(1, plan.group[p]):
                a_copy(p, k, d).wait_send()
            for e in range(1, plan.adds[p]):
                b_copy(p, k, e).wait_send()
            for d in range(1, R):
                c_copy(p, k, d).wait_send()
    for d in range(1, T):
        d_copy(d).wait_send()
    for d in range(1, R):
        e_copy(d).wait_send()


def shards(features, row_salt, column_multiplier, column_offset, thresholds):
    users, columns = features.shape
    plan = Plan(lax.axis_size("rows"), lax.axis_size("tiles"), users, columns)
    R, T, K, width, CT, RB = plan.rows, plan.tiles, plan.pieces, plan.width, plan.tile_cols, plan.tile_rows
    f32, vmem = jnp.float32, pltpu.VMEM
    G, U = plan.group, plan.adds

    def pair(make):
        return [make(0), make(1)]

    def sems(*shape):
        return [pltpu.SemaphoreType.DMA(shape)] * 2

    scratch = (
        [vmem((users, 1), jnp.int32), vmem((users, WIN), f32)]
        + pair(lambda p: vmem((G[p], users, WIN), f32))
        + pair(lambda p: vmem((WIN, G[p] * users), jnp.bfloat16))
        + pair(lambda p: vmem((K, G[p] - 1, users, U[p] * width), f32))
        + pair(lambda p: vmem((K, G[p] * users, U[p] * width), f32))
        + pair(lambda p: vmem((K, U[p], WIN, width), f32))
        + pair(lambda p: vmem((K, U[p] - 1, WIN, width), f32))
        + [vmem((2, K, WIN, width), f32), vmem((2, K, R - 1, RB, width), f32)]
        + [vmem((T, 1, CT + WIN), f32), vmem((T - 1, 1, CT + WIN), f32)]
        + [vmem((1, CT + WIN), f32), vmem((R - 1, 1, CT + WIN), f32)]
        + sems(G[0] + G[1] - 2)
        + sems(K, G[0] - 1) + sems(K, G[1] - 1)
        + sems(K, U[0] - 1) + sems(K, U[1] - 1)
        + sems(2, K, R - 1) + sems(T - 1) + sems(R - 1)
    )
    spec = pl.BlockSpec(memory_space=pltpu.VMEM)
    gram, query_norms, column_norms = pl.pallas_call(
        functools.partial(kernel, plan),
        out_shape=(
            jax.ShapeDtypeStruct((RB, CT), f32),
            jax.ShapeDtypeStruct((RB, 1), f32),
            jax.ShapeDtypeStruct((1, CT), f32),
        ),
        in_specs=[spec] * 5,
        out_specs=(spec,) * 3,
        scratch_shapes=scratch,
        compiler_params=pltpu.CompilerParams(
            collective_id=0, has_side_effects=True, vmem_limit_bytes=60 * 1024 * 1024
        ),
        name="similarity",
    )(
        features,
        row_salt.reshape(1, users),
        column_multiplier.reshape(1, columns),
        column_offset.reshape(1, columns),
        thresholds.reshape(1, columns),
    )
    return gram / (query_norms * column_norms)


def solution(mesh):
    placed = (P(("rows", "tiles"), None), P(("rows", "tiles")), P(), P(), P())
    return jax.shard_map(
        shards, mesh=mesh, in_specs=placed, out_specs=P("rows", "tiles"), check_vma=False
    )
```

```python
import functools

import jax
import jax.numpy as jnp
from jax import lax
from jax.experimental import pallas as pl
from jax.experimental.pallas import tpu as pltpu
from jax.sharding import PartitionSpec as P

WIN = 256
PRIME = 65521
AHEAD = 2
MESH = pl.DeviceIdType.MESH


class Plan:
    def __init__(self, rows, tiles, users, columns):
        self.rows, self.tiles, self.users, self.columns = rows, tiles, users, columns
        self.outer, self.inner = 2, tiles // 2
        self.tile_cols = columns // tiles
        self.tile_rows = WIN // rows
        self.width = 128
        units = self.tile_cols // self.width
        self.pieces = max(1, (units - 4) // 4)
        self.sub = self.pieces * self.width
        self.rest = (self.tile_cols - 4 * self.sub) // 2
        self.group = (2 * self.inner, 2 * self.outer)
        self.adds = (self.outer, self.inner)


def fold(h):
    return (h >> 16) * 15 + (h & 65535)


def kernel(
    plan, feat_hbm, salt, mult, offset, thr, out,
    feat, saltc, q0, q1, qt0, qt1, s0, s1, r0, r1, p0, p1, g0, g1, acc, fin,
    zs, zr, zpart, zfin, zsum, zgot, sq, sqr, sqa, sqf,
    feat_sem, q_send, q_recv, a_send0, a_recv0, a_send1, a_recv1, b_send0, b_recv0, b_send1, b_recv1,
    c_send, c_recv, d_send, d_recv, e_send, e_recv, z_send, z_recv, y_send, y_recv, t_send, t_recv,
):
    R, T, users, width, K = plan.rows, plan.tiles, plan.users, plan.width, plan.pieces
    A, B, CT, sub, RB, rest = plan.outer, plan.inner, plan.tile_cols, plan.sub, plan.tile_rows, plan.rest
    chips = (B, A)
    adds = plan.adds
    r, t = lax.axis_index("rows"), lax.axis_index("tiles")
    c = lax.rem(r, 2)
    base = r - c
    partner = (base + 1 - c, t)
    a, b = t // B, lax.rem(t, B)
    q_in, qt, s, rc, part, got = (q0, q1), (qt0, qt1), (s0, s1), (r0, r1), (p0, p1), (g0, g1)
    a_sem, b_sem = ((a_send0, a_recv0), (a_send1, a_recv1)), ((b_send0, b_recv0), (b_send1, b_recv1))

    feat_copy = pltpu.make_async_copy(feat_hbm, feat, feat_sem.at[0])
    feat_copy.start()
    barrier = pltpu.get_barrier_semaphore()
    for d in range(1, 2 * T):
        other = lax.rem(t * 2 + c + d, 2 * T)
        pl.semaphore_signal(
            barrier, inc=1, device_id=(base + lax.rem(other, 2), other // 2), device_id_type=MESH
        )
    for d in range(1, R):
        pl.semaphore_signal(barrier, inc=1, device_id=(lax.rem(r + d, R), t), device_id_type=MESH)

    def along(p, j):
        return lax.rem(b + j, B) if p == 0 else lax.rem(a + j, A)

    def member(p, j, core):
        return (base + core, a * B + along(p, j) if p == 0 else along(p, j) * B + b)

    def core_of(other):
        return 1 - c if other else c

    def adder(p, e):
        if p == 0:
            return (r, lax.rem(a + e, A) * B + b)
        return (r, a * B + lax.rem(b + e, B))

    def remote(src, dst, send, recv, to):
        return pltpu.make_async_remote_copy(
            src_ref=src, dst_ref=dst, send_sem=send, recv_sem=recv, device_id=to, device_id_type=MESH
        )

    def targets(p):
        return [(j, other) for j in range(chips[p]) for other in (0, 1) if j or other]

    def q_copy(p, j, to):
        slot = 2 * j + c
        return lambda src_slot, sem: remote(
            q_in[p].at[src_slot], q_in[p].at[slot], q_send.at[p, sem], q_recv.at[p, slot], to
        )

    def q_direct(p, j):
        return q_copy(p, j, member(p, j, c))(c, 2 * j)

    def q_onchip(p, j):
        return q_copy(p, j, partner)(2 * j + c, 2 * j + 1)

    def q_wait(p, j, core):
        slot = 2 * j + core
        remote(q_in[p].at[slot], q_in[p].at[slot], q_send.at[p, slot], q_recv.at[p, slot], partner).wait_recv()

    def a_copy(p, k, j, other):
        slot = 2 * j + c
        return remote(
            s[p].at[k, 2 * j + other],
            rc[p].at[k, pl.ds(pl.multiple_of(slot * users, users), users)],
            a_sem[p][0].at[k, 2 * j + other], a_sem[p][1].at[k, slot], member(p, j, core_of(other)),
        )

    def a_wait(p, k, j, other):
        slot = 2 * j + core_of(other)
        remote(
            s[p].at[k, 2 * j + other],
            rc[p].at[k, pl.ds(pl.multiple_of(slot * users, users), users)],
            a_sem[p][0].at[k, 2 * j + other], a_sem[p][1].at[k, slot], partner,
        ).wait_recv()

    def b_copy(p, k, e):
        return remote(
            part[p].at[k, e], got[p].at[k, e - 1], b_sem[p][0].at[k, e - 1], b_sem[p][1].at[k, e - 1], adder(p, e)
        )

    def rows_of(other):
        return pl.ds(pl.multiple_of(other * RB, RB), RB)

    def c_copy(p, k, d):
        other = lax.rem(r + d, R)
        return remote(
            acc.at[p, k, rows_of(other)], fin.at[p, k, d - 1],
            c_send.at[p, k, d - 1], c_recv.at[p, k, d - 1], (other, t),
        )

    def d_copy(d):
        other = lax.rem(t + d, T)
        return remote(sq.at[other], sqr.at[d - 1], d_send.at[d - 1], d_recv.at[d - 1], (r, other))

    def e_copy(d):
        return remote(sqa, sqf.at[d - 1], e_send.at[d - 1], e_recv.at[d - 1], (lax.rem(r + d, R), t))

    def z_copy():
        return remote(
            zs, zr.at[pl.ds(pl.multiple_of(c * users, users), users)], z_send.at[0], z_recv.at[0], partner
        )

    def y_copy(d):
        other = lax.rem(r + d, R)
        return remote(
            zpart.at[rows_of(other)], zfin.at[d - 1], y_send.at[d - 1], y_recv.at[d - 1], (other, t)
        )

    def t_copy(d):
        other = lax.rem(t + d, T)
        return remote(zsum.at[other], zgot.at[d - 1], t_send.at[d - 1], t_recv.at[d - 1], (r, other))

    step = min(users, 64)

    def sample(start, size, store):
        cols = pl.ds(pl.multiple_of(start, 128), size)
        by, plus, limit = mult[:, cols], offset[:, cols], thr[:, cols]
        weight = lax.rsqrt(limit.astype(jnp.float32) / float(PRIME))

        def body(i, total):
            rows = pl.ds(pl.multiple_of(i * step, step), step)
            x = feat[rows, cols].astype(jnp.float32)
            h = fold(fold(saltc[rows, :] * by + plus))
            h = jnp.where(h >= PRIME, h - PRIME, h)
            value = x * weight
            store(pl.multiple_of(i * step, step), jnp.where(h < limit, value, jnp.zeros_like(value)))
            return total + jnp.sum((x * x).reshape(step // 8, 8, size), axis=0)

        total = lax.fori_loop(0, users // step, body, jnp.zeros((8, size), jnp.float32))
        return jnp.sum(total, axis=0, keepdims=True)

    def sample_for(p, k, chip, core, store):
        for e in range(adds[p]):
            if p == 0:
                tile = lax.rem(a + e, A) * B + chip
            else:
                tile = chip * B + lax.rem(b + e, B)
            inside = (2 * p + core) * sub + k * width
            squares = sample(tile * CT + inside, width, functools.partial(store, e))
            sq[tile, :, pl.ds(pl.multiple_of(inside, 128), width)] = squares

    def gather_piece(k):
        def keep(p, row0, e, row, value):
            rc[p][k, pl.ds(row0 + row, step), pl.ds(e * width, width)] = value

        def away(p, slot, e, row, value):
            s[p][k, slot, pl.ds(row, step), pl.ds(e * width, width)] = value

        for j, other in sorted(set(targets(0) + targets(1)), key=lambda x: (x[0] == 0, x)):
            for p in range(2):
                if j < chips[p]:
                    sample_for(p, k, along(p, j), core_of(other), functools.partial(away, p, 2 * j + other))
                    a_copy(p, k, j, other).start()
        for p in range(2):
            sample_for(p, k, along(p, 0), c, functools.partial(keep, p, pl.multiple_of(c * users, users)))

    def sample_rest(core, store):
        def tile_body(tile, _):
            inside = 4 * sub + core * rest
            squares = sample(
                tile * CT + inside, rest, functools.partial(store, pl.multiple_of(tile * rest, 128))
            )
            sq[tile, :, pl.ds(pl.multiple_of(inside, 128), rest)] = squares
            return 0

        lax.fori_loop(0, T, tile_body, 0)

    diagonal = lax.broadcasted_iota(jnp.int32, (users, users), 0) == lax.broadcasted_iota(
        jnp.int32, (users, users), 1
    )
    spread = jnp.where(diagonal, jnp.broadcast_to(salt[...].astype(jnp.float32), (users, users)), 0.0)
    saltc[...] = jnp.sum(spread, axis=1, keepdims=True).astype(jnp.int32)

    def store_q(row, value):
        for p in range(2):
            q_in[p][c, pl.ds(row, step), :] = value

    feat_copy.wait()
    q_squares = sample(0, WIN, store_q)
    for tile in range(T):
        sq[tile, :, pl.ds(CT, WIN)] = q_squares
    pl.semaphore_wait(barrier, 2 * T - 1 + R - 1)

    for p in range(2):
        for j in range(1, chips[p]):
            q_direct(p, j).start()
    for p in range(2):
        q_onchip(p, 0).start()
    gather_piece(0)

    def store_zs(col, row, value):
        zs[pl.ds(row, step), pl.ds(col, rest)] = value

    def store_zr(col, row, value):
        zr[pl.ds(pl.multiple_of(c * users, users) + row, step), pl.ds(col, rest)] = value

    def turn(p, slot):
        return q_in[p][slot].T.astype(jnp.bfloat16)

    sample_rest(1 - c, store_zs)
    z_copy().start()
    sample_rest(c, store_zr)
    for k in range(1, min(AHEAD, K)):
        gather_piece(k)
    for p in range(2):
        q_wait(p, 0, 1 - c)
        for slot in range(2):
            qt[p][:, pl.ds(slot * users, users)] = turn(p, slot)
    for p in range(2):
        for j in range(1, chips[p]):
            q_wait(p, j, c)
            q_onchip(p, j).start()
    z_copy().wait_recv()
    for tile in range(T):
        cols = pl.ds(tile * rest, rest)
        zpart[:, cols] = jnp.dot(
            qt[0][:, pl.ds(0, 2 * users)], zr[:, cols].astype(jnp.bfloat16), preferred_element_type=jnp.float32
        )
    for d in range(1, R):
        y_copy(d).start()
    for p in range(2):
        for j in range(1, chips[p]):
            q_wait(p, j, 1 - c)
            for slot in (2 * j, 2 * j + 1):
                qt[p][:, pl.ds(slot * users, users)] = turn(p, slot)

    for k in range(K + 1):
        if k < K:
            for p in range(2):
                for j, other in targets(p):
                    a_wait(p, k, j, other)
                product = jnp.dot(
                    qt[p][...], rc[p][k].astype(jnp.bfloat16), preferred_element_type=jnp.float32
                )
                for e in list(range(1, adds[p])) + [0]:
                    part[p][k, e] = product[:, e * width : (e + 1) * width]
                    if e:
                        b_copy(p, k, e).start()
        if k + AHEAD < K:
            gather_piece(k + AHEAD)
        if k == max(0, K - 1 - AHEAD):
            for d in range(1, T):
                d_copy(d).start()
        if k == K - 1:
            for d in range(1, T):
                t_copy(d).start()
        if k >= 1:
            for p in range(2):
                total = part[p][k - 1, 0]
                for e in range(1, adds[p]):
                    b_copy(p, k - 1, e).wait_recv()
                    total = total + got[p][k - 1, e - 1]
                acc[p, k - 1] = total
                for d in range(1, R):
                    c_copy(p, k - 1, d).start()
        if k == max(0, K - 2):
            same, cross = zpart[rows_of(r)], None
            for d in range(1, R):
                y_copy(d).wait_recv()
                if d % 2 == 0:
                    same = same + zfin[d - 1]
                else:
                    cross = zfin[d - 1] if cross is None else cross + zfin[d - 1]
            for tile in range(T):
                zsum[tile, rows_of(c)] = same[:, tile * rest : (tile + 1) * rest]
                zsum[tile, rows_of(1 - c)] = cross[:, tile * rest : (tile + 1) * rest]
        if k == K - 1:
            total = sq[t]
            for d in range(1, T):
                d_copy(d).wait_recv()
                total = total + sqr[d - 1]
            sqa[...] = total
            for d in range(1, R):
                e_copy(d).start()

    squares = sqa[...]
    for d in range(1, R):
        e_copy(d).wait_recv()
        squares = squares + sqf[d - 1]
    norms = jnp.sqrt(squares + 1e-06)
    sqa_mine = lax.broadcasted_iota(jnp.int32, (RB, WIN), 1) == r * RB + lax.broadcasted_iota(
        jnp.int32, (RB, WIN), 0
    )
    query_norms = jnp.sum(
        jnp.where(sqa_mine, jnp.broadcast_to(norms[:, CT:], (RB, WIN)), 0.0), axis=1, keepdims=True
    )
    sqr[0] = norms

    def put(start, value):
        cols = pl.ds(pl.multiple_of(start, 128), value.shape[1])
        out[:, cols] = value / (query_norms * sqr[0, :, cols])

    total = zsum[t]
    for d in range(1, T):
        t_copy(d).wait_recv()
        total = total + zgot[d - 1]
    for core in range(2):
        put(4 * sub + core * rest, total[core * RB : (core + 1) * RB])

    for k in range(K):
        for p in range(2):
            same, cross = acc[p, k, rows_of(r)], None
            for d in range(1, R):
                c_copy(p, k, d).wait_recv()
                piece = fin[p, k, d - 1]
                if d % 2 == 0:
                    same = same + piece
                else:
                    cross = piece if cross is None else cross + piece
            put((2 * p + c) * sub + k * width, same)
            put((2 * p + 1 - c) * sub + k * width, cross)

    for p in range(2):
        for j in range(chips[p]):
            if j:
                q_direct(p, j).wait_send()
            q_onchip(p, j).wait_send()
    z_copy().wait_send()
    for k in range(K):
        for p in range(2):
            for j, other in targets(p):
                a_copy(p, k, j, other).wait_send()
            for e in range(1, adds[p]):
                b_copy(p, k, e).wait_send()
            for d in range(1, R):
                c_copy(p, k, d).wait_send()
    for d in range(1, T):
        d_copy(d).wait_send()
        t_copy(d).wait_send()
    for d in range(1, R):
        e_copy(d).wait_send()
        y_copy(d).wait_send()


def shards(features, row_salt, column_multiplier, column_offset, thresholds):
    users, columns = features.shape
    plan = Plan(lax.axis_size("rows"), lax.axis_size("tiles"), users, columns)
    R, T, K, width, CT, RB = plan.rows, plan.tiles, plan.pieces, plan.width, plan.tile_cols, plan.tile_rows
    f32, vmem = jnp.float32, pltpu.VMEM
    G, U = plan.group, plan.adds

    def pair(make):
        return [make(0), make(1)]

    def sems(*shape):
        return [pltpu.SemaphoreType.DMA(shape)] * 2

    rest = plan.rest
    scratch = (
        [vmem((users, columns), features.dtype), vmem((users, 1), jnp.int32)]
        + pair(lambda p: vmem((G[p], users, WIN), f32))
        + pair(lambda p: vmem((WIN, G[p] * users), jnp.bfloat16))
        + pair(lambda p: vmem((K, G[p], users, U[p] * width), f32))
        + pair(lambda p: vmem((K, G[p] * users, U[p] * width), f32))
        + pair(lambda p: vmem((K, U[p], WIN, width), f32))
        + pair(lambda p: vmem((K, U[p] - 1, WIN, width), f32))
        + [vmem((2, K, WIN, width), f32), vmem((2, K, R - 1, RB, width), f32)]
        + [vmem((users, T * rest), f32), vmem((2 * users, T * rest), f32), vmem((WIN, T * rest), f32)]
        + [vmem((R - 1, RB, T * rest), f32), vmem((T, 2 * RB, rest), f32), vmem((T - 1, 2 * RB, rest), f32)]
        + [vmem((T, 1, CT + WIN), f32), vmem((T - 1, 1, CT + WIN), f32)]
        + [vmem((1, CT + WIN), f32), vmem((R - 1, 1, CT + WIN), f32)]
        + [pltpu.SemaphoreType.DMA((1,))]
        + sems(2, max(G))
        + sems(K, G[0]) + sems(K, G[1])
        + sems(K, U[0] - 1) + sems(K, U[1] - 1)
        + sems(2, K, R - 1) + sems(T - 1) + sems(R - 1)
        + sems(1) + sems(R - 1) + sems(T - 1)
    )
    spec = pl.BlockSpec(memory_space=pltpu.VMEM)
    return pl.pallas_call(
        functools.partial(kernel, plan),
        out_shape=jax.ShapeDtypeStruct((RB, CT), f32),
        in_specs=[pl.BlockSpec(memory_space=pl.ANY)] + [spec] * 4,
        out_specs=spec,
        scratch_shapes=scratch,
        compiler_params=pltpu.CompilerParams(
            collective_id=0, has_side_effects=True, vmem_limit_bytes=60 * 1024 * 1024
        ),
        name="similarity",
    )(
        features,
        row_salt.reshape(1, users),
        column_multiplier.reshape(1, columns),
        column_offset.reshape(1, columns),
        thresholds.reshape(1, columns),
    )


def solution(mesh):
    placed = (P(("rows", "tiles"), None), P(("rows", "tiles")), P(), P(), P())
    return jax.shard_map(
        shards, mesh=mesh, in_specs=placed, out_specs=P("rows", "tiles"), check_vma=False
    )
```

```python
import functools

import jax
import jax.numpy as jnp
from jax import lax
from jax.experimental import pallas as pl
from jax.experimental.pallas import tpu as pltpu
from jax.sharding import PartitionSpec as P

WIN = 256
PRIME = 65521
AHEAD = 2
MESH = pl.DeviceIdType.MESH


class Plan:
    def __init__(self, rows, tiles, users, columns):
        self.rows, self.tiles, self.users, self.columns = rows, tiles, users, columns
        self.outer, self.inner = 2, tiles // 2
        self.tile_cols = columns // tiles
        self.tile_rows = WIN // rows
        self.width = 128
        units = self.tile_cols // self.width
        self.pieces = max(1, (units - 4) // 4)
        self.sub = self.pieces * self.width
        self.rest = (self.tile_cols - 4 * self.sub) // 2
        self.group = (2 * self.inner, 2 * self.outer)
        self.adds = (self.outer, self.inner)


def fold(h):
    return (h >> 16) * 15 + (h & 65535)


def kernel(
    plan, feat_hbm, salt, mult, offset, thr, out,
    feat, saltc, q0, q1, qt0, qt1, s0, s1, r0, r1, p0, p1, g0, g1, acc, fin,
    zs, zr, zpart, zfin, zsum, zgot, sq, sqr, sqa, sqf,
    feat_sem, q_send, q_recv, a_send0, a_recv0, a_send1, a_recv1, b_send0, b_recv0, b_send1, b_recv1,
    c_send, c_recv, d_send, d_recv, e_send, e_recv, z_send, z_recv, y_send, y_recv, t_send, t_recv,
):
    R, T, users, width, K = plan.rows, plan.tiles, plan.users, plan.width, plan.pieces
    A, B, CT, sub, RB, rest = plan.outer, plan.inner, plan.tile_cols, plan.sub, plan.tile_rows, plan.rest
    chips = (B, A)
    adds = plan.adds
    r, t = lax.axis_index("rows"), lax.axis_index("tiles")
    c = lax.rem(r, 2)
    base = r - c
    partner = (base + 1 - c, t)
    a, b = t // B, lax.rem(t, B)
    q_in, qt, s, rc, part, got = (q0, q1), (qt0, qt1), (s0, s1), (r0, r1), (p0, p1), (g0, g1)
    a_sem, b_sem = ((a_send0, a_recv0), (a_send1, a_recv1)), ((b_send0, b_recv0), (b_send1, b_recv1))

    feat_copy = pltpu.make_async_copy(feat_hbm, feat, feat_sem.at[0])
    feat_copy.start()
    barrier = pltpu.get_barrier_semaphore()
    for d in range(1, 2 * T):
        other = lax.rem(t * 2 + c + d, 2 * T)
        pl.semaphore_signal(
            barrier, inc=1, device_id=(base + lax.rem(other, 2), other // 2), device_id_type=MESH
        )
    for d in range(1, R):
        pl.semaphore_signal(barrier, inc=1, device_id=(lax.rem(r + d, R), t), device_id_type=MESH)

    def along(p, j):
        return lax.rem(b + j, B) if p == 0 else lax.rem(a + j, A)

    def member(p, j, core):
        return (base + core, a * B + along(p, j) if p == 0 else along(p, j) * B + b)

    def core_of(other):
        return 1 - c if other else c

    def adder(p, e):
        if p == 0:
            return (r, lax.rem(a + e, A) * B + b)
        return (r, a * B + lax.rem(b + e, B))

    def remote(src, dst, send, recv, to):
        return pltpu.make_async_remote_copy(
            src_ref=src, dst_ref=dst, send_sem=send, recv_sem=recv, device_id=to, device_id_type=MESH
        )

    def targets(p):
        return [(j, other) for j in range(chips[p]) for other in (0, 1) if j or other]

    def q_copy(p, j, to):
        slot = 2 * j + c
        return lambda src_slot, sem: remote(
            q_in[p].at[src_slot], q_in[p].at[slot], q_send.at[p, sem], q_recv.at[p, slot], to
        )

    def q_direct(p, j):
        return q_copy(p, j, member(p, j, c))(c, 2 * j)

    def q_onchip(p, j):
        return q_copy(p, j, partner)(2 * j + c, 2 * j + 1)

    def q_wait(p, j, core):
        slot = 2 * j + core
        remote(q_in[p].at[slot], q_in[p].at[slot], q_send.at[p, slot], q_recv.at[p, slot], partner).wait_recv()

    def a_copy(p, k, j, other):
        slot = 2 * j + c
        return remote(
            s[p].at[k, 2 * j + other],
            rc[p].at[k, pl.ds(pl.multiple_of(slot * users, users), users)],
            a_sem[p][0].at[k, 2 * j + other], a_sem[p][1].at[k, slot], member(p, j, core_of(other)),
        )

    def a_wait(p, k, j, other):
        slot = 2 * j + core_of(other)
        remote(
            s[p].at[k, 2 * j + other],
            rc[p].at[k, pl.ds(pl.multiple_of(slot * users, users), users)],
            a_sem[p][0].at[k, 2 * j + other], a_sem[p][1].at[k, slot], partner,
        ).wait_recv()

    def b_copy(p, k, e):
        return remote(
            part[p].at[k, e], got[p].at[k, e - 1], b_sem[p][0].at[k, e - 1], b_sem[p][1].at[k, e - 1], adder(p, e)
        )

    def rows_of(other):
        return pl.ds(pl.multiple_of(other * RB, RB), RB)

    def c_copy(p, k, d):
        other = lax.rem(r + d, R)
        return remote(
            acc.at[p, k, rows_of(other)], fin.at[p, k, d - 1],
            c_send.at[p, k, d - 1], c_recv.at[p, k, d - 1], (other, t),
        )

    def d_copy(d):
        other = lax.rem(t + d, T)
        return remote(sq.at[other], sqr.at[d - 1], d_send.at[d - 1], d_recv.at[d - 1], (r, other))

    def e_copy(d):
        return remote(sqa, sqf.at[d - 1], e_send.at[d - 1], e_recv.at[d - 1], (lax.rem(r + d, R), t))

    def z_copy():
        return remote(
            zs, zr.at[pl.ds(pl.multiple_of(c * users, users), users)], z_send.at[0], z_recv.at[0], partner
        )

    def y_copy(d):
        other = lax.rem(r + d, R)
        return remote(
            zpart.at[rows_of(other)], zfin.at[d - 1], y_send.at[d - 1], y_recv.at[d - 1], (other, t)
        )

    def t_copy(d):
        other = lax.rem(t + d, T)
        return remote(zsum.at[other], zgot.at[d - 1], t_send.at[d - 1], t_recv.at[d - 1], (r, other))

    step = min(users, 64)

    def sample(start, size, store):
        cols = pl.ds(pl.multiple_of(start, 128), size)
        by, plus, limit = mult[:, cols], offset[:, cols], thr[:, cols]
        weight = lax.rsqrt(limit.astype(jnp.float32) / float(PRIME))

        def body(i, total):
            rows = pl.ds(pl.multiple_of(i * step, step), step)
            x = feat[rows, cols].astype(jnp.float32)
            h = fold(fold(saltc[rows, :] * by + plus))
            h = jnp.where(h >= PRIME, h - PRIME, h)
            value = x * weight
            store(pl.multiple_of(i * step, step), jnp.where(h < limit, value, jnp.zeros_like(value)))
            return total + jnp.sum((x * x).reshape(step // 8, 8, size), axis=0)

        total = lax.fori_loop(0, users // step, body, jnp.zeros((8, size), jnp.float32))
        return jnp.sum(total, axis=0, keepdims=True)

    def sample_for(p, k, chip, core, store):
        for e in range(adds[p]):
            if p == 0:
                tile = lax.rem(a + e, A) * B + chip
            else:
                tile = chip * B + lax.rem(b + e, B)
            inside = (2 * p + core) * sub + k * width
            squares = sample(tile * CT + inside, width, functools.partial(store, e))
            sq[tile, :, pl.ds(pl.multiple_of(inside, 128), width)] = squares

    def gather_piece(k):
        def keep(p, row0, e, row, value):
            rc[p][k, pl.ds(row0 + row, step), pl.ds(e * width, width)] = value

        def away(p, slot, e, row, value):
            s[p][k, slot, pl.ds(row, step), pl.ds(e * width, width)] = value

        for j, other in sorted(set(targets(0) + targets(1)), key=lambda x: (x[0] == 0, x)):
            for p in range(2):
                if j < chips[p]:
                    sample_for(p, k, along(p, j), core_of(other), functools.partial(away, p, 2 * j + other))
                    a_copy(p, k, j, other).start()
        for p in range(2):
            sample_for(p, k, along(p, 0), c, functools.partial(keep, p, pl.multiple_of(c * users, users)))

    def sample_rest(core, store):
        def tile_body(tile, _):
            inside = 4 * sub + core * rest
            squares = sample(
                tile * CT + inside, rest, functools.partial(store, pl.multiple_of(tile * rest, 128))
            )
            sq[tile, :, pl.ds(pl.multiple_of(inside, 128), rest)] = squares
            return 0

        lax.fori_loop(0, T, tile_body, 0)

    diagonal = lax.broadcasted_iota(jnp.int32, (users, users), 0) == lax.broadcasted_iota(
        jnp.int32, (users, users), 1
    )
    spread = jnp.where(diagonal, jnp.broadcast_to(salt[...].astype(jnp.float32), (users, users)), 0.0)
    saltc[...] = jnp.sum(spread, axis=1, keepdims=True).astype(jnp.int32)

    def store_q(row, value):
        for p in range(2):
            q_in[p][c, pl.ds(row, step), :] = value

    feat_copy.wait()
    q_squares = sample(0, WIN, store_q)
    for tile in range(T):
        sq[tile, :, pl.ds(CT, WIN)] = q_squares
    pl.semaphore_wait(barrier, 2 * T - 1 + R - 1)

    for p in range(2):
        for j in range(1, chips[p]):
            q_direct(p, j).start()
    for p in range(2):
        q_onchip(p, 0).start()
    gather_piece(0)

    def store_zs(col, row, value):
        zs[pl.ds(row, step), pl.ds(col, rest)] = value

    def store_zr(col, row, value):
        zr[pl.ds(pl.multiple_of(c * users, users) + row, step), pl.ds(col, rest)] = value

    def turn(p, slot):
        return q_in[p][slot].T.astype(jnp.bfloat16)

    sample_rest(1 - c, store_zs)
    z_copy().start()
    sample_rest(c, store_zr)
    for k in range(1, min(AHEAD, K)):
        gather_piece(k)
    for p in range(2):
        q_wait(p, 0, 1 - c)
        for slot in range(2):
            qt[p][:, pl.ds(slot * users, users)] = turn(p, slot)
    for p in range(2):
        for j in range(1, chips[p]):
            q_wait(p, j, c)
            q_onchip(p, j).start()
    z_copy().wait_recv()
    for tile in range(T):
        cols = pl.ds(tile * rest, rest)
        zpart[:, cols] = jnp.dot(
            qt[0][:, pl.ds(0, 2 * users)], zr[:, cols].astype(jnp.bfloat16), preferred_element_type=jnp.float32
        )
    for d in range(1, R):
        y_copy(d).start()
    for p in range(2):
        for j in range(1, chips[p]):
            q_wait(p, j, 1 - c)
            for slot in (2 * j, 2 * j + 1):
                qt[p][:, pl.ds(slot * users, users)] = turn(p, slot)

    for k in range(K + 1):
        if k < K:
            for p in range(2):
                for j, other in targets(p):
                    a_wait(p, k, j, other)
                product = jnp.dot(
                    qt[p][...], rc[p][k].astype(jnp.bfloat16), preferred_element_type=jnp.float32
                )
                for e in list(range(1, adds[p])) + [0]:
                    part[p][k, e] = product[:, e * width : (e + 1) * width]
                    if e:
                        b_copy(p, k, e).start()
        if k + AHEAD < K:
            gather_piece(k + AHEAD)
        if k == max(0, K - 1 - AHEAD):
            for d in range(1, T):
                d_copy(d).start()
        if k == K - 1:
            for d in range(1, T):
                t_copy(d).start()
        if k >= 1:
            for p in range(2):
                total = part[p][k - 1, 0]
                for e in range(1, adds[p]):
                    b_copy(p, k - 1, e).wait_recv()
                    total = total + got[p][k - 1, e - 1]
                acc[p, k - 1] = total
                for d in range(1, R):
                    c_copy(p, k - 1, d).start()
        if k == max(0, K - 2):
            same, cross = zpart[rows_of(r)], None
            for d in range(1, R):
                y_copy(d).wait_recv()
                if d % 2 == 0:
                    same = same + zfin[d - 1]
                else:
                    cross = zfin[d - 1] if cross is None else cross + zfin[d - 1]
            for tile in range(T):
                zsum[tile, rows_of(c)] = same[:, tile * rest : (tile + 1) * rest]
                zsum[tile, rows_of(1 - c)] = cross[:, tile * rest : (tile + 1) * rest]
        if k == max(0, K - 2):
            total = sq[t]
            for d in range(1, T):
                d_copy(d).wait_recv()
                total = total + sqr[d - 1]
            sqa[...] = total
            for d in range(1, R):
                e_copy(d).start()

    squares = sqa[...]
    for d in range(1, R):
        e_copy(d).wait_recv()
        squares = squares + sqf[d - 1]
    norms = jnp.sqrt(squares + 1e-06)
    sqa_mine = lax.broadcasted_iota(jnp.int32, (RB, WIN), 1) == r * RB + lax.broadcasted_iota(
        jnp.int32, (RB, WIN), 0
    )
    query_norms = jnp.sum(
        jnp.where(sqa_mine, jnp.broadcast_to(norms[:, CT:], (RB, WIN)), 0.0), axis=1, keepdims=True
    )
    sqr[0] = norms

    def put(start, value):
        cols = pl.ds(pl.multiple_of(start, 128), value.shape[1])
        out[:, cols] = value / (query_norms * sqr[0, :, cols])

    total = zsum[t]
    for d in range(1, T):
        t_copy(d).wait_recv()
        total = total + zgot[d - 1]
    for core in range(2):
        put(4 * sub + core * rest, total[core * RB : (core + 1) * RB])

    for k in range(K):
        for p in range(2):
            same, cross = acc[p, k, rows_of(r)], None
            for d in range(1, R):
                c_copy(p, k, d).wait_recv()
                piece = fin[p, k, d - 1]
                if d % 2 == 0:
                    same = same + piece
                else:
                    cross = piece if cross is None else cross + piece
            put((2 * p + c) * sub + k * width, same)
            put((2 * p + 1 - c) * sub + k * width, cross)

    for p in range(2):
        for j in range(chips[p]):
            if j:
                q_direct(p, j).wait_send()
            q_onchip(p, j).wait_send()
    z_copy().wait_send()
    for k in range(K):
        for p in range(2):
            for j, other in targets(p):
                a_copy(p, k, j, other).wait_send()
            for e in range(1, adds[p]):
                b_copy(p, k, e).wait_send()
            for d in range(1, R):
                c_copy(p, k, d).wait_send()
    for d in range(1, T):
        d_copy(d).wait_send()
        t_copy(d).wait_send()
    for d in range(1, R):
        e_copy(d).wait_send()
        y_copy(d).wait_send()


def shards(features, row_salt, column_multiplier, column_offset, thresholds):
    users, columns = features.shape
    plan = Plan(lax.axis_size("rows"), lax.axis_size("tiles"), users, columns)
    R, T, K, width, CT, RB = plan.rows, plan.tiles, plan.pieces, plan.width, plan.tile_cols, plan.tile_rows
    f32, vmem = jnp.float32, pltpu.VMEM
    G, U = plan.group, plan.adds

    def pair(make):
        return [make(0), make(1)]

    def sems(*shape):
        return [pltpu.SemaphoreType.DMA(shape)] * 2

    rest = plan.rest
    scratch = (
        [vmem((users, columns), features.dtype), vmem((users, 1), jnp.int32)]
        + pair(lambda p: vmem((G[p], users, WIN), f32))
        + pair(lambda p: vmem((WIN, G[p] * users), jnp.bfloat16))
        + pair(lambda p: vmem((K, G[p], users, U[p] * width), f32))
        + pair(lambda p: vmem((K, G[p] * users, U[p] * width), f32))
        + pair(lambda p: vmem((K, U[p], WIN, width), f32))
        + pair(lambda p: vmem((K, U[p] - 1, WIN, width), f32))
        + [vmem((2, K, WIN, width), f32), vmem((2, K, R - 1, RB, width), f32)]
        + [vmem((users, T * rest), f32), vmem((2 * users, T * rest), f32), vmem((WIN, T * rest), f32)]
        + [vmem((R - 1, RB, T * rest), f32), vmem((T, 2 * RB, rest), f32), vmem((T - 1, 2 * RB, rest), f32)]
        + [vmem((T, 1, CT + WIN), f32), vmem((T - 1, 1, CT + WIN), f32)]
        + [vmem((1, CT + WIN), f32), vmem((R - 1, 1, CT + WIN), f32)]
        + [pltpu.SemaphoreType.DMA((1,))]
        + sems(2, max(G))
        + sems(K, G[0]) + sems(K, G[1])
        + sems(K, U[0] - 1) + sems(K, U[1] - 1)
        + sems(2, K, R - 1) + sems(T - 1) + sems(R - 1)
        + sems(1) + sems(R - 1) + sems(T - 1)
    )
    spec = pl.BlockSpec(memory_space=pltpu.VMEM)
    return pl.pallas_call(
        functools.partial(kernel, plan),
        out_shape=jax.ShapeDtypeStruct((RB, CT), f32),
        in_specs=[pl.BlockSpec(memory_space=pl.ANY)] + [spec] * 4,
        out_specs=spec,
        scratch_shapes=scratch,
        compiler_params=pltpu.CompilerParams(
            collective_id=0, has_side_effects=True, vmem_limit_bytes=60 * 1024 * 1024
        ),
        name="similarity",
    )(
        features,
        row_salt.reshape(1, users),
        column_multiplier.reshape(1, columns),
        column_offset.reshape(1, columns),
        thresholds.reshape(1, columns),
    )


def solution(mesh):
    placed = (P(("rows", "tiles"), None), P(("rows", "tiles")), P(), P(), P())
    return jax.shard_map(
        shards, mesh=mesh, in_specs=placed, out_specs=P("rows", "tiles"), check_vma=False
    )
```
